128 devices in a mesh: req: 4 (over x), hid: 32 (over y, z, core).
Axes of the slice: x: 4, y: 4, z: 4, core: 2. Of those that a mesh axis runs over, the one named last changes fastest.
Arguments:
- layer_input: bfloat16 [2048, 7168], P('req', 'hid'), may hold values from -6 to 6
- norm_gain: float32 [7168], replicated, may hold values from 0.1 to 1.9
- qkv_weight: bfloat16 [7168, 21504], P('req', 'hid'), may hold values from -0.09375 to 0.09375
- cache_keys: bfloat16 [4, 4096, 7168], P('req', None, 'hid'), may hold values from -160 to 160
- cache_values: bfloat16 [4, 4096, 7168], P('req', None, 'hid'), may hold values from -8 to 8
- cache_lengths: int32 [4], P('req'), may hold values from 1 to 4096, 10240 in all
- out_weight: bfloat16 [7168, 3584], P('hid'), may hold values from -0.375 to 0.375
- mlp_gain: float32 [3584], replicated, may hold values from 0.1 to 1.9
- gate_weight: bfloat16 [3584, 14336], P(None, 'hid'), may hold values from -0.09375 to 0.09375
- up_weight: bfloat16 [3584, 14336], P(None, 'hid'), may hold values from -0.09375 to 0.09375
- down_weight: bfloat16 [14336, 3584], P('hid'), may hold values from -0.046875 to 0.046875
Outputs:
- block_out: bfloat16 [2048, 3584], P(('req', 'hid'))
The draws below stay inside these ranges and needn't reach their ends.
All inputs are finite; a program needn't handle non-finite values. No bound on the sum of `cache_lengths` on one device may be relied on, other than what follows from the above.
Results may differ from the reference program's by a relative error of at most 0.02.
Values may be sent and summed in bfloat16 or wider, within the bound.
A program may use at most 128 MiB of HBM per device.

```python
import math
import jax
import jax.numpy as jnp
import numpy as np
from jax import lax

D = 3584
FF = 14336
H = 32
HD = 224
SPAN = 512
CACHE = 4096
REQS = 4
TOKENS = 2048


def draw_cache_keys(key, part):
    key_base = jax.random.fold_in(jax.random.fold_in(key, 17), 0)
    shape = (REQS, CACHE, H * HD)
    keys = 1.4 * jax.random.normal(key_base, shape, jnp.float32)
    return jnp.clip(keys, -160.0, 160.0).astype(jnp.bfloat16)


def block_levels(stream_key, extent, shards, low, largest):
    loudness = 1.0
    for dim, shards_of in shards:
        heights = jax.random.uniform(jax.random.fold_in(jax.random.fold_in(stream_key, 6), dim), (shards_of,), jnp.float32, low / len(shards), largest / len(shards))
        loudness = loudness * jnp.repeat(jnp.exp(heights), extent[dim] // shards_of).reshape((-1,) + (1,) * (len(extent) - 1 - dim))
    return loudness


def length_profile(count, total, most, skew):
    portions = [(1 << 20) // math.isqrt(rank ** skew) + 1 for rank in range(2, count + 1)]
    surplus, holding = total - most - (count - 1), [1] * (count - 1)
    while surplus > 0:
        candidates = [i for i in range(count - 1) if holding[i] < most]
        mass, budget = sum([portions[i] for i in candidates]), surplus
        for i in candidates:
            more = min(most - holding[i], max(1, budget * portions[i] // mass), surplus)
            holding[i] = holding[i] + more
            surplus = surplus - more
    return np.array([most] + holding)


def ragged(key, number_of, total, limit, slope):
    if number_of == 2:
        one = jax.random.randint(key, (), max(1, total - limit), min(limit, total - 1) + 1)
        return jnp.stack([one, total - one])
    sizes = jnp.asarray(length_profile(number_of, total, limit, slope), jnp.int32)
    couples = (number_of - 1) // 2
    source_of, taker = sizes[1:1 + 2 * couples:2], sizes[2:2 + 2 * couples:2]
    margin = jnp.minimum(source_of - 1, limit - taker)
    shifted = jax.random.randint(jax.random.fold_in(key, 1), (couples,), 0, 1 << 20) % (margin + 1)
    sizes = sizes.at[1:1 + 2 * couples:2].set(source_of - shifted).at[2:2 + 2 * couples:2].set(taker + shifted)
    return sizes[jax.random.permutation(jax.random.fold_in(key, 2), number_of)]


def centred(rng, extent, spread, reach, cuts=(), held_as=jnp.bfloat16):
    drawn = jax.random.normal(rng, extent, jnp.float32) * spread
    if len(cuts) > 0:
        drawn = block_levels(rng, extent, cuts, -0.22, 0.18) * drawn
    return jnp.clip(drawn, min=-reach, max=reach).astype(held_as)


def setup_inputs(seed: int = 0) -> dict:
    key_list = jax.random.split(jax.random.key(seed), 12)
    layer_input = centred(key_list[0], (TOKENS, 2 * D), 1.0, 6.0, ((0, 4), (1, 32)))
    norm_gain = jnp.clip(1.0 + 0.18 * jax.random.normal(key_list[1], (2 * D,), jnp.float32), 0.1, 1.9)
    qkv_weight = centred(key_list[2], (2 * D, 3 * H * HD), D ** -0.5, 0.09375, ((0, 4), (1, 32)))
    cache_keys = draw_cache_keys(jax.random.fold_in(key_list[11], 71), 0)
    cache_values = centred(key_list[4], (REQS, CACHE, H * HD), 1.4, 8.0, ((0, 4), (2, 32)))
    cache_lengths = ragged(key_list[5], REQS, CACHE * (REQS + 1) // 2, CACHE, 2).astype(jnp.int32)
    out_weight = centred(key_list[6], (H * HD, D), HD ** -0.5, 0.375, ((0, 32),))
    mlp_gain = jnp.clip(1.0 + 0.18 * jax.random.normal(key_list[7], (D,), jnp.float32), 0.1, 1.9)
    gate_weight = centred(key_list[8], (D, FF), D ** -0.5, 0.09375, ((1, 32),))
    up_weight = centred(key_list[9], (D, FF), D ** -0.5, 0.09375, ((1, 32),))
    down_weight = centred(key_list[10], (FF, D), FF ** -0.5, 0.046875, ((0, 32),))
    return {"layer_input": layer_input, "norm_gain": norm_gain, "qkv_weight": qkv_weight, "cache_keys": cache_keys, "cache_values": cache_values, "cache_lengths": cache_lengths, "out_weight": out_weight, "mlp_gain": mlp_gain, "gate_weight": gate_weight, "up_weight": up_weight, "down_weight": down_weight}


epsilon = 1e-05

def rms_scale(values, gain):
    return values * lax.rsqrt(lax.optimization_barrier(jnp.mean(values * values, axis=-1, keepdims=True)) + epsilon) * gain

def rotate(values, position):
    half = values.shape[-1] // 2
    freq = jnp.exp(-jnp.log(10000.0) * 2.0 * jnp.arange(half, dtype=jnp.float32) / values.shape[-1])
    angle = position.astype(jnp.float32)[:, None, None] * freq[None, None, :]
    cosine = jnp.cos(angle)
    sine = jnp.sin(angle)
    first = values[..., :half]
    second = values[..., half:]
    return jnp.concatenate([first * cosine - second * sine, second * cosine + first * sine], axis=-1)

def attend(query, keys, values, length):
    scores = jnp.dot(query, keys.T, preferred_element_type=jnp.float32) * HD ** (-0.5)
    rows = jnp.arange(SPAN, dtype=jnp.int32)[:, None]
    cols = jnp.arange(CACHE + SPAN, dtype=jnp.int32)[None, :]
    valid = jnp.where(cols < CACHE, cols < length, cols - CACHE <= rows)
    scores = jnp.where(valid, scores, -1e+30)
    top = lax.optimization_barrier(jnp.max(scores, axis=1, keepdims=True))
    weights = jnp.exp(scores - top)
    total = lax.optimization_barrier(jnp.sum(weights, axis=1, keepdims=True))
    mixed = jnp.dot(weights.astype(jnp.bfloat16), values, preferred_element_type=jnp.float32)
    return (mixed / total).astype(jnp.bfloat16)

def reference(layer_input, norm_gain, qkv_weight, cache_keys, cache_values, cache_lengths, out_weight, mlp_gain, gate_weight, up_weight, down_weight):
    normed = rms_scale(layer_input.astype(jnp.float32), norm_gain).astype(jnp.bfloat16)
    projected = jnp.dot(normed, qkv_weight, preferred_element_type=jnp.float32).reshape(TOKENS, H, 3, HD)
    position = (cache_lengths[:, None] + jnp.arange(SPAN, dtype=jnp.int32)[None, :]).reshape(TOKENS)
    query = rotate(projected[:, :, 0], position).astype(jnp.bfloat16)
    fresh_keys = rotate(projected[:, :, 1], position).astype(jnp.bfloat16)
    fresh_values = projected[:, :, 2].astype(jnp.bfloat16)
    all_keys = jnp.concatenate([cache_keys.reshape(REQS, CACHE, H, HD), fresh_keys.reshape(REQS, SPAN, H, HD)], axis=1)
    all_values = jnp.concatenate([cache_values.reshape(REQS, CACHE, H, HD), fresh_values.reshape(REQS, SPAN, H, HD)], axis=1)
    all_keys = jnp.transpose(all_keys, (0, 2, 1, 3)).reshape(REQS * H, CACHE + SPAN, HD)
    all_values = jnp.transpose(all_values, (0, 2, 1, 3)).reshape(REQS * H, CACHE + SPAN, HD)
    queries = jnp.transpose(query.reshape(REQS, SPAN, H, HD), (0, 2, 1, 3)).reshape(REQS * H, SPAN, HD)
    lengths = jnp.repeat(cache_lengths, H)
    mixed = lax.map(lambda item: attend(item[0], item[1], item[2], item[3]), (queries, all_keys, all_values, lengths))
    heads_out = jnp.transpose(mixed.reshape(REQS, H, SPAN, HD), (0, 2, 1, 3)).reshape(TOKENS, H * HD)
    attention = jnp.dot(heads_out, out_weight, preferred_element_type=jnp.float32)
    mid = (layer_input[:, :D].astype(jnp.float32) + attention).astype(jnp.bfloat16)
    mlp_in = rms_scale(mid.astype(jnp.float32), mlp_gain).astype(jnp.bfloat16)
    gate = jnp.dot(mlp_in, gate_weight, preferred_element_type=jnp.float32)
    upward = jnp.dot(mlp_in, up_weight, preferred_element_type=jnp.float32)
    hidden = (jax.nn.gelu(gate, approximate=True) * upward).astype(jnp.bfloat16)
    downward = jnp.dot(hidden, down_weight, preferred_element_type=jnp.float32)
    return (mid.astype(jnp.float32) + downward).astype(jnp.bfloat16)
```

```python
import jax
import jax.numpy as jnp
from jax import lax
from jax.experimental import pallas as pl
from jax.experimental.pallas import tpu as pltpu
from jax.sharding import PartitionSpec as P

D = 3584
HD = 224
MESH = pl.DeviceIdType.MESH
epsilon = 1e-05
F32 = jnp.float32
BF16 = jnp.bfloat16
CHUNKS = 4
CW = D // CHUNKS
HALF = D // 2


def rms_scale(values, gain):
    return values * lax.rsqrt(jnp.mean(values * values, axis=-1, keepdims=True) + epsilon) * gain


class Net:
    def __init__(self, send_sems, recv_sems):
        self.send_sems, self.recv_sems, self.used = send_sems, recv_sems, 0
        self.started = []

    def copy(self, src, dst, device):
        n = self.used
        self.used += 1
        op = pltpu.make_async_remote_copy(
            src_ref=src,
            dst_ref=dst,
            send_sem=self.send_sems.at[n],
            recv_sem=self.recv_sems.at[n],
            device_id=device,
            device_id_type=MESH,
        )
        op.start()
        self.started.append(op)
        return op

    def drain(self):
        for op in self.started:
            op.wait_send()
        self.started = []


def ring(value, step):
    return (value + step) % 4


def place():
    row = lax.axis_index("req")
    hid = lax.axis_index("hid")
    return row, hid // 8, (hid // 2) % 4, hid % 2


def reduce_scatter(net, partial, bufs):
    row, y, z, c = place()
    out_ref, in_ref, s_ref, t1_ref, t2_ref, s1_ref, t3_ref = bufs

    def first_axis(k, pos):
        return (row, pos * 8 + z * 2 + c) if k % 2 == 0 else (row, y * 8 + pos * 2 + c)

    def second_axis(k, pos):
        return (row, y * 8 + pos * 2 + c) if k % 2 == 0 else (row, pos * 8 + z * 2 + c)

    pair = []
    for k in range(CHUNKS):
        out_ref[k] = partial(1 - c, k).astype(BF16)
        pair.append(net.copy(out_ref.at[k], in_ref.at[k], (row, y * 8 + z * 2 + 1 - c)))
    relay = []
    straight = []
    for k in range(CHUNKS):
        u = y if k % 2 == 0 else z
        mine = partial(c, k)
        pair[k].wait_recv()
        total = (mine + in_ref[k].astype(F32)).astype(BF16)
        for a in range(4):
            for b in range(4):
                rows = total[(a * 4 + b) * 16 : (a * 4 + b + 1) * 16]
                if k % 2 == 0:
                    s_ref[k, a, b] = rows
                else:
                    s_ref[k, b, a] = rows
        far, near = [], []
        for way in range(2):
            nb = ring(u, 1 if way == 0 else 3)
            ha, hb = (0, 2) if way == 0 else (2, 0)
            target = first_axis(k, nb)
            far.append(net.copy(s_ref.at[k, ring(u, 2), pl.ds(ha, 2)], t1_ref.at[k, way], target))
            near.append(net.copy(s_ref.at[k, nb, pl.ds(hb, 2)], t2_ref.at[k, way, pl.ds(hb, 2)], target))
        relay.append(far)
        straight.append(near)
    closing = []
    for k in range(CHUNKS):
        u = y if k % 2 == 0 else z
        ends = []
        for way in range(2):
            nb = ring(u, 1 if way == 0 else 3)
            ha = 0 if way == 0 else 2
            relay[k][way].wait_recv()
            s_ref[k, nb, pl.ds(ha, 2)] = (
                s_ref[k, nb, pl.ds(ha, 2)].astype(F32) + t1_ref[k, way].astype(F32)
            ).astype(BF16)
            ends.append(
                net.copy(s_ref.at[k, nb, pl.ds(ha, 2)], t2_ref.at[k, way, pl.ds(ha, 2)], first_axis(k, nb))
            )
        closing.append(ends)
    last = []
    for k in range(CHUNKS):
        u, w = (y, z) if k % 2 == 0 else (z, y)
        for way in range(2):
            straight[k][way].wait_recv()
            closing[k][way].wait_recv()
        s1_ref[k] = (
            s_ref[k, u].astype(F32) + t2_ref[k, 0].astype(F32) + t2_ref[k, 1].astype(F32)
        ).astype(BF16)
        sends = []
        for step in range(1, 4):
            peer = ring(w, step)
            sends.append(net.copy(s1_ref.at[k, peer], t3_ref.at[k, step - 1], second_axis(k, peer)))
        last.append(sends)
    result = []
    for k in range(CHUNKS):
        w = z if k % 2 == 0 else y
        value = s1_ref[k, w].astype(F32)
        for step in range(3):
            last[k][step].wait_recv()
            value = value + t3_ref[k, step].astype(F32)
        result.append(value)
    return jnp.concatenate(result, axis=1)


def all_gather(net, m_ref):
    row, y, z, c = place()
    here = m_ref.at[y, z, c]
    first = []
    for half in range(2):
        cols = pl.ds(half * HALF, HALF)
        sends = []
        for step in range(1, 4):
            device = (row, y * 8 + ring(z, step) * 2 + c) if half == 0 else (row, ring(y, step) * 8 + z * 2 + c)
            sends.append(net.copy(here.at[:, cols], here.at[:, cols], device))
        first.append(sends)

    def block(half, u, lo, count):
        cols = pl.ds(half * HALF, HALF)
        if half == 0:
            return m_ref.at[u, pl.ds(lo, count), c, :, cols]
        return m_ref.at[pl.ds(lo, count), u, c, :, cols]

    def device(half, u):
        return (row, u * 8 + z * 2 + c) if half == 0 else (row, y * 8 + u * 2 + c)

    partner = (row, y * 8 + z * 2 + 1 - c)
    near, far, swap = [], [], []
    for half in range(2):
        u = y if half == 0 else z
        for op in first[half]:
            op.wait_recv()
        near.append([net.copy(block(half, u, 0, 4), block(half, u, 0, 4), device(half, ring(u, s))) for s in (1, 3)])
    for half in range(2):
        u = y if half == 0 else z
        swap.append(net.copy(block(half, u, 0, 4), block(half, u, 0, 4), partner))
    for half in range(2):
        u = y if half == 0 else z
        ends = []
        for way in range(2):
            near[half][way].wait_recv()
            source = ring(u, 3 if way == 0 else 1)
            lo = 0 if way == 0 else 2
            ends.append(
                net.copy(
                    block(half, source, lo, 2), block(half, source, lo, 2), device(half, ring(u, 1 if way == 0 else 3))
                )
            )
            swap.append(net.copy(block(half, source, 0, 4), block(half, source, 0, 4), partner))
        far.append(ends)
    for half in range(2):
        u = y if half == 0 else z
        for op in far[half]:
            op.wait_recv()
        swap.append(net.copy(block(half, ring(u, 2), 0, 4), block(half, ring(u, 2), 0, 4), partner))
    for op in swap:
        op.wait_recv()


def post_kernel(
    heads_hbm, x_hbm, shift_hbm, ow_hbm, gain_ref, gw_hbm, uw_hbm, dw_hbm,
    out_ref,
    heads, x, shift, ow, gw, uw, dw, m_ref, hidden,
    p_out, p_in, s_ref, t1, t2, s1, t3,
    send_sems, recv_sems, local_sems,
):
    row, y, z, c = place()
    loads = []
    for n, (src, dst) in enumerate(
        [(heads_hbm, heads), (ow_hbm, ow), (x_hbm, x), (shift_hbm, shift), (gw_hbm, gw), (uw_hbm, uw), (dw_hbm, dw)]
    ):
        op = pltpu.make_async_copy(src, dst, local_sems.at[n])
        op.start()
        loads.append(op)
    barrier = pltpu.get_barrier_semaphore()
    peers = [(row, y * 8 + z * 2 + 1 - c)]
    for step in range(1, 4):
        peers.append((row, ring(y, step) * 8 + z * 2 + c))
        peers.append((row, y * 8 + ring(z, step) * 2 + c))
    for peer in peers:
        pl.semaphore_signal(barrier, inc=1, device_id=peer, device_id_type=MESH)
    pl.semaphore_wait(barrier, len(peers))

    net = Net(send_sems, recv_sems)
    for n in range(4):
        loads[n].wait()

    def bufs(n):
        return tuple(ref.at[n] for ref in (p_out, p_in, s_ref, t1, t2, s1, t3))

    def attention_part(core, k):
        cols = pl.ds(k * CW, CW)
        return jnp.dot(
            heads[:, core].reshape(256, HD), ow[:, cols], preferred_element_type=F32
        ) + jnp.dot(x[:, core].reshape(256, HD), shift[:, cols], preferred_element_type=F32)

    mid = reduce_scatter(net, attention_part, bufs(0)).astype(BF16).astype(F32)
    m_ref[y, z, c] = rms_scale(mid, gain_ref[...]).astype(BF16)
    all_gather(net, m_ref)
    loads[4].wait()
    loads[5].wait()

    @pl.loop(0, 2)
    def _(i):
        rows = m_ref[pl.ds(2 * i, 2)].reshape(256, D)
        gate = jnp.dot(rows, gw[...], preferred_element_type=F32)
        upward = jnp.dot(rows, uw[...], preferred_element_type=F32)
        hidden[pl.ds(8 * i, 8)] = (jax.nn.gelu(gate, approximate=True) * upward).astype(BF16).reshape(8, 2, 16, 448)

    loads[6].wait()

    def mlp_part(core, k):
        return jnp.dot(
            hidden[:, core].reshape(256, 448), dw[:, pl.ds(k * CW, CW)], preferred_element_type=F32
        )

    total = reduce_scatter(net, mlp_part, bufs(1))
    out_ref[...] = (mid + total).astype(BF16)
    net.drain()


def post(heads_out, x, shift, out_weight, mlp_gain, gate_weight, up_weight, down_weight):
    anywhere = pl.BlockSpec(memory_space=pl.ANY)
    vmem = pl.BlockSpec(memory_space=pltpu.VMEM)
    copies = 2 * CHUNKS * 10 + 22
    return pl.pallas_call(
        post_kernel,
        out_shape=jax.ShapeDtypeStruct((16, D), BF16),
        in_specs=[anywhere, anywhere, anywhere, anywhere, vmem, anywhere, anywhere, anywhere],
        out_specs=vmem,
        scratch_shapes=[
            pltpu.VMEM((16, 2, 16, HD), BF16),
            pltpu.VMEM((16, 2, 16, HD), BF16),
            pltpu.VMEM((HD, D), BF16),
            pltpu.VMEM((HD, D), BF16),
            pltpu.VMEM((D, 448), BF16),
            pltpu.VMEM((D, 448), BF16),
            pltpu.VMEM((448, D), BF16),
            pltpu.VMEM((4, 4, 2, 16, D), BF16),
            pltpu.VMEM((16, 2, 16, 448), BF16),
            pltpu.VMEM((2, CHUNKS, 256, CW), BF16),
            pltpu.VMEM((2, CHUNKS, 256, CW), BF16),
            pltpu.VMEM((2, CHUNKS, 4, 4, 16, CW), BF16),
            pltpu.VMEM((2, CHUNKS, 2, 2, 16, CW), BF16),
            pltpu.VMEM((2, CHUNKS, 2, 4, 16, CW), BF16),
            pltpu.VMEM((2, CHUNKS, 4, 16, CW), BF16),
            pltpu.VMEM((2, CHUNKS, 3, 16, CW), BF16),
            pltpu.SemaphoreType.DMA((copies,)),
            pltpu.SemaphoreType.DMA((copies,)),
            pltpu.SemaphoreType.DMA((7,)),
        ],
        compiler_params=pltpu.CompilerParams(
            collective_id=1, has_side_effects=True, vmem_limit_bytes=58 * 1024 * 1024
        ),
        name="post_attention",
    )(
        heads_out.reshape(16, 2, 16, HD), x.reshape(16, 2, 16, HD), shift, out_weight,
        mlp_gain.reshape(1, D), gate_weight, up_weight, down_weight,
    )


def rotate(values, position):
    half = values.shape[-1] // 2
    freq = jnp.exp(-jnp.log(10000.0) * 2.0 * jnp.arange(half, dtype=jnp.float32) / values.shape[-1])
    angle = position.astype(jnp.float32)[:, None, None] * freq[None, None, :]
    cosine = jnp.cos(angle)
    sine = jnp.sin(angle)
    first = values[..., :half]
    second = values[..., half:]
    return jnp.concatenate(
        [first * cosine - second * sine, second * cosine + first * sine], axis=-1
    )


def merge_block(carry, scores, values):
    top, total, accum = carry
    new_top = jnp.maximum(top, jnp.max(scores, axis=2))
    fade = jnp.exp(top - new_top)
    weights = jnp.exp(scores - new_top[:, :, None])
    total = total * fade + jnp.sum(weights, axis=2)
    accum = accum * fade.T[:, :, None] + jnp.einsum(
        "hqk,khd->qhd", weights.astype(jnp.bfloat16), values, preferred_element_type=jnp.float32
    )
    return (new_top, total, accum)


def shards(
    layer_input, norm_gain, qkv_weight, cache_keys, cache_values, cache_lengths,
    out_weight, mlp_gain, gate_weight, up_weight, down_weight,
):
    span = layer_input.shape[0]
    heads_dev = cache_keys.shape[2] // HD
    slots = cache_keys.shape[1]
    scale = HD ** (-0.5)
    whole_input = lax.all_gather(layer_input, "hid", axis=1, tiled=True)
    normed = rms_scale(whole_input.astype(jnp.float32), norm_gain).astype(jnp.bfloat16)
    projected = jnp.dot(
        normed,
        lax.all_gather(qkv_weight, "req", axis=0, tiled=True),
        preferred_element_type=jnp.float32,
    ).reshape(span, heads_dev, 3, HD)
    length = cache_lengths[0]
    position = length + jnp.arange(span, dtype=jnp.int32)
    query = rotate(projected[:, :, 0], position).astype(jnp.bfloat16)
    fresh_keys = rotate(projected[:, :, 1], position).astype(jnp.bfloat16)
    fresh_values = projected[:, :, 2].astype(jnp.bfloat16)
    cache_k = cache_keys[0].reshape(slots, heads_dev, HD)
    cache_v = cache_values[0].reshape(slots, heads_dev, HD)
    block = min(512, slots)
    block_count = (length + block - 1) // block

    def visit(index, carry):
        keys = lax.dynamic_slice_in_dim(cache_k, index * block, block, 0)
        values = lax.dynamic_slice_in_dim(cache_v, index * block, block, 0)
        scores = jnp.einsum("qhd,khd->hqk", query, keys, preferred_element_type=jnp.float32) * scale
        columns = index * block + jnp.arange(block, dtype=jnp.int32)
        scores = jnp.where(columns[None, None, :] < length, scores, -1e30)
        return merge_block(carry, scores, values)

    start_state = (
        jnp.full((heads_dev, span), -1e30, jnp.float32),
        jnp.zeros((heads_dev, span), jnp.float32),
        jnp.zeros((span, heads_dev, HD), jnp.float32),
    )
    state = lax.fori_loop(0, block_count, visit, start_state)
    fresh_scores = (
        jnp.einsum("qhd,khd->hqk", query, fresh_keys, preferred_element_type=jnp.float32) * scale
    )
    causal = (
        jnp.arange(span, dtype=jnp.int32)[None, :] <= jnp.arange(span, dtype=jnp.int32)[:, None]
    )
    fresh_scores = jnp.where(causal[None, :, :], fresh_scores, -1e30)
    top, total, accum = merge_block(state, fresh_scores, fresh_values)
    heads_out = (accum / total.T[:, :, None]).astype(jnp.bfloat16).reshape(span, heads_dev * HD)
    start = lax.axis_index("hid") * HD
    shift = (
        jnp.arange(D, dtype=jnp.int32)[None, :] == start + jnp.arange(HD, dtype=jnp.int32)[:, None]
    ).astype(BF16)
    return post(heads_out, layer_input, shift, out_weight, mlp_gain, gate_weight, up_weight, down_weight)


def solution(mesh):
    placed = (
        P("req", "hid"),
        P(),
        P("req", "hid"),
        P("req", None, "hid"),
        P("req", None, "hid"),
        P("req"),
        P("hid", None),
        P(),
        P(None, "hid"),
        P(None, "hid"),
        P("hid", None),
    )
    return jax.shard_map(
        shards, mesh=mesh, in_specs=placed, out_specs=P(("req", "hid"), None), check_vma=False
    )
```
